32 devices in a mesh: mode: 2 (over x), scan: 16 (over z, y, core).
Axes of the slice: x: 2, y: 2, z: 4, core: 2. Of those that a mesh axis runs over, the one named last changes fastest.
Arguments:
- object_field: float32 [2, 8192, 1024], P(None, 'scan'), may hold values from -4.2 to 4.2
- probe: bfloat16 [2, 12, 512, 512], P(None, 'mode'), may hold values from -1.796875 to 1.796875
- patterns: float32 [16, 512, 512], P('scan'), may hold values from 0.2 to 6
- row_shift: int32 [16], P('scan'), may hold values from 0 to 1
- col_start: int32 [16], P('scan'), may hold values from 0 to 2
- mixing: int32 [12, 12], replicated, may hold values from -5 to 20, as said below
Outputs:
- object_new: float32 [2, 8192, 1024], P(None, 'scan')
- probe_new: bfloat16 [2, 12, 512, 512], P(None, 'mode', 'scan')
The draws below stay inside these ranges and needn't reach their ends.
Inputs may be any that keep to these rules, and one draw needn't show every extreme that they name: `mixing`: diagonal entries are 12 to 20, the others -5 to 5.
All inputs are finite; a program needn't handle non-finite values.
Results may differ from the reference program's by a relative error of at most 0.0095.
The reference program's roundings to bfloat16 on the way count: a program that leaves them out, or rounds other values in their place, can miss the bound.
Values sent between devices are 32-bit elements; how exact they have to be, the bound alone decides.
A program may use at most 128 MiB of HBM per device.

```python
import math
import jax
import jax.numpy as jnp
from jax import lax

TILE = 512
MODES = 12
OBJ_COLS = 1024
P_DEV = 1
HALF = 256
POS = 16
OBJ_ROWS = 8192


def draw_mixing(key, part):
    first_key, second_key = jax.random.split(jax.random.fold_in(key, 7))
    off_values = jax.random.randint(first_key, (MODES, MODES), -5, 6, dtype=jnp.int32)
    diag_values = jax.random.randint(second_key, (MODES,), 12, 21, dtype=jnp.int32)
    identity = jnp.eye(MODES, dtype=jnp.int32)
    return off_values * (1 - identity) + diag_values[:, None] * identity


def place_ends(drawn, key, least, top_value):
    extent = drawn.shape
    spot = [jax.random.randint(jax.random.fold_in(key, axis), (), 0, extent[axis]) for axis in range(len(extent))]
    drawn = drawn.at[tuple(spot)].set(least)
    longest = extent.index(max(extent))
    spot[longest] = (spot[longest] + 1) % extent[longest]
    return drawn.at[tuple(spot)].set(top_value)


def steps_of(stream_key, extent, shards, smallest, top_value):
    def one(dim, shards_of):
        heights = jax.random.uniform(jax.random.fold_in(jax.random.fold_in(stream_key, 6), dim), (shards_of,), jnp.float32, smallest / len(shards), top_value / len(shards))
        return jnp.repeat(jnp.exp(heights), extent[dim] // shards_of).reshape((-1,) + (1,) * (len(extent) - dim - 1))

    gain = one(*shards[0])
    for cut in shards[1:]:
        gain = gain * one(*cut)
    return gain


def scatter_about(own_key, dims, width, limit, pieces=(), kind=jnp.bfloat16):
    entries = jax.random.normal(own_key, dims, jnp.float32) * width
    if len(pieces) > 0:
        entries = steps_of(own_key, dims, pieces, -0.22, 0.18) * entries
    return jnp.clip(entries, min=-limit, max=limit).astype(kind)


def setup_inputs(seed: int = 0) -> dict:
    keys = jax.random.split(jax.random.key(seed), 7)
    object_field = scatter_about(keys[0], (2, OBJ_ROWS, OBJ_COLS), 0.7, 4.2, ((1, 16),), jnp.float32)
    probe = scatter_about(keys[1], (2, MODES, TILE, TILE), 0.3, 1.796875, ((1, 2),))
    patterns = jnp.clip(jnp.exp(math.log(6.0) - 3.4011974 * jax.random.uniform(keys[2], (POS, TILE, TILE), jnp.float32) ** steps_of(keys[2], (POS, TILE, TILE), ((0, 16),), -0.2, 0.2)), 0.2, 6.0)
    row_shift = place_ends(jax.random.randint(keys[3], (POS,), 0, 2), jax.random.fold_in(keys[3], 1), 0, 1).astype(jnp.int32)
    col_start = place_ends(jax.random.randint(keys[4], (POS,), 0, 2 * OBJ_COLS // TILE - 1), jax.random.fold_in(keys[4], 1), 0, (2 * OBJ_COLS // TILE - 1) - 1).astype(jnp.int32)
    mixing = draw_mixing(jax.random.fold_in(keys[6], 71), 0)
    return {"object_field": object_field, "probe": probe, "patterns": patterns, "row_shift": row_shift, "col_start": col_start, "mixing": mixing}


def tables(tile_size):
    indices = jnp.arange(tile_size, dtype=jnp.int32)
    products = indices[:, None] * indices[None, :] % tile_size
    angles = products.astype(jnp.float32) * (2.0 * math.pi / tile_size)
    factor = 1.0 / math.sqrt(tile_size)
    return ((jnp.cos(angles) * factor).astype(jnp.bfloat16), (jnp.sin(angles) * factor).astype(jnp.bfloat16))

def right_mult(first, second):
    return jnp.einsum('...ij,jk->...ik', first.astype(jnp.float32), second.astype(jnp.float32))

def left_mult(first, second):
    return jnp.einsum('ij,...jk->...ik', first.astype(jnp.float32), second.astype(jnp.float32))

def transform(real_part, imag_part, cosine, sine_table, direction):
    half_real = right_mult(real_part, cosine) - direction * right_mult(imag_part, sine_table)
    half_imag = right_mult(imag_part, cosine) + direction * right_mult(real_part, sine_table)
    half_real = half_real.astype(jnp.bfloat16)
    half_imag = half_imag.astype(jnp.bfloat16)
    out_real = left_mult(cosine, half_real) - direction * left_mult(sine_table, half_imag)
    out_imag = left_mult(cosine, half_imag) + direction * left_mult(sine_table, half_real)
    return (out_real, out_imag)

def reference(object_field, probe, patterns, row_shift, col_start, mixing):
    cosine, sine_table = tables(TILE)
    padded = jnp.pad(object_field, ((0, 0), (0, HALF), (0, 0)))
    probe_real = probe[0].astype(jnp.float32)
    probe_imag = probe[1].astype(jnp.float32)
    illumination = lax.optimization_barrier(jnp.sum(probe_real * probe_real + probe_imag * probe_imag, axis=0))

    def visit(carry, inputs):
        object_grad, probe_grad = carry
        position, pattern, shift_rows, column = inputs
        row_first = (position // P_DEV * TILE + shift_rows * HALF).astype(jnp.int32)
        col_first = (column * HALF).astype(jnp.int32)
        zero_index = jnp.zeros((), jnp.int32)
        patches = lax.dynamic_slice(padded, (zero_index, row_first, col_first), (2, TILE, TILE))
        obj_real = patches[0]
        obj_imag = patches[1]
        exit_real = (probe_real * obj_real - probe_imag * obj_imag).astype(jnp.bfloat16)
        exit_imag = (probe_real * obj_imag + probe_imag * obj_real).astype(jnp.bfloat16)
        wave_real, wave_imag = transform(exit_real, exit_imag, cosine, sine_table, -1.0)
        summed = lax.optimization_barrier(jnp.sum(wave_real * wave_real + wave_imag * wave_imag, axis=0))
        scaling = jnp.sqrt(pattern) / jnp.sqrt(jnp.maximum(summed, 1.0))
        fixed_real = (wave_real * scaling).astype(jnp.bfloat16)
        fixed_imag = (wave_imag * scaling).astype(jnp.bfloat16)
        back_real, back_imag = transform(fixed_real, fixed_imag, cosine, sine_table, 1.0)
        resid_real = back_real - exit_real.astype(jnp.float32)
        resid_imag = back_imag - exit_imag.astype(jnp.float32)
        grad_real = lax.optimization_barrier(jnp.sum(probe_real * resid_real + probe_imag * resid_imag, axis=0))
        grad_imag = lax.optimization_barrier(jnp.sum(probe_real * resid_imag - probe_imag * resid_real, axis=0))
        region = lax.dynamic_slice(object_grad, (zero_index, row_first, col_first), (2, TILE, TILE))
        region = region + jnp.stack([grad_real, grad_imag])
        object_grad = lax.dynamic_update_slice(object_grad, region, (zero_index, row_first, col_first))
        step_real = obj_real * resid_real + obj_imag * resid_imag
        step_imag = obj_real * resid_imag - obj_imag * resid_real
        probe_grad = probe_grad + jnp.stack([step_real, step_imag])
        return ((object_grad, probe_grad), None)
    start_object = jnp.zeros((2, OBJ_ROWS + HALF, OBJ_COLS), jnp.float32)
    start_probe = jnp.zeros((2, MODES, TILE, TILE), jnp.float32)
    inputs = (jnp.arange(POS, dtype=jnp.int32), patterns, row_shift, col_start)
    (object_grad, probe_grad), unused = lax.scan(visit, (start_object, start_probe), inputs)
    object_new = object_field + object_grad[:, :OBJ_ROWS, :] / jnp.max(illumination)
    updated = probe.astype(jnp.float32) + probe_grad / math.sqrt(POS)
    weights = mixing.astype(jnp.float32) / 16.0
    probe_new = jnp.einsum('kj,cjrt->ckrt', weights, updated, precision=lax.Precision.HIGHEST)
    return (object_new, probe_new.astype(jnp.bfloat16))
```

```python
import functools
import math

import jax
import jax.numpy as jnp
import numpy as np
from jax import lax
from jax.experimental import pallas as pl
from jax.experimental.pallas import tpu as pltpu
from jax.sharding import PartitionSpec as P

BF16 = jnp.bfloat16
F32 = jnp.float32


def tables(tile_size):
    indices = np.arange(tile_size)
    products = indices[:, None] * indices[None, :] % tile_size
    angles = products * (2.0 * math.pi / tile_size)
    factor = 1.0 / math.sqrt(tile_size)
    cosine = (np.cos(angles).astype(np.float32) * np.float32(factor)).astype(BF16)
    sine = (np.sin(angles).astype(np.float32) * np.float32(factor)).astype(BF16)
    return cosine, sine


def kernel(
    dims,
    shift_ref, col_ref, mix_ref,
    obj, probe, rows_in, pat, cos_t, sin_t,
    delta, probe_new,
    rim, patch, t1, t2, half, big, recv1, recv2, recv3,
    light, light_in, own_sum, peer_sum, down_in, upd, upd_in, lmax,
    rim_sem, light_sem, sum_sem, sem1, sem2, sem3, sem4, down_sem, out_sem, table_sem,
):
    n, group, share, tile, modes, positions, cols = dims
    hb = tile // 2
    quarter = tile // 4
    me = lax.axis_index("mode")
    idx = lax.axis_index("scan")
    a = idx % 2
    b = (idx // 2) % 2
    m = idx // 4
    other = 1 - me
    sib = idx + 1 - 2 * a
    yid = idx + 2 - 4 * b
    nxt = (idx + 1) % n
    prv = (idx + n - 1) % n

    def remote(src, dst, sems, mode, scan):
        return pltpu.make_async_remote_copy(
            src_ref=src, dst_ref=dst, send_sem=sems[0], recv_sem=sems[1],
            device_id=(mode, scan), device_id_type=pl.DeviceIdType.MESH,
        )

    front, back = pl.ds(0, tile), pl.ds(tile, tile)
    table_copies = [
        pltpu.make_async_copy(cos_t, t1.at[front, front], table_sem.at[0]),
        pltpu.make_async_copy(cos_t, t1.at[back, back], table_sem.at[1]),
        pltpu.make_async_copy(sin_t, t1.at[back, front], table_sem.at[2]),
    ]
    for copy in table_copies:
        copy.start()

    partners = [(other, idx), (me, sib), (me, yid), (me, nxt), (me, prv)]
    partners += [(me, ((m + j) % group) * 4 + b * 2 + a) for j in range(1, group)]
    barrier = pltpu.get_barrier_semaphore()
    for partner in partners:
        pl.semaphore_signal(barrier, inc=1, device_id=partner, device_id_type=pl.DeviceIdType.MESH)
    pl.semaphore_wait(barrier, len(partners))

    rim_copy = remote(obj.at[:, pl.ds(0, hb), :], rim, (rim_sem.at[0], rim_sem.at[1]), me, prv)
    rim_copy.start()

    for h in range(2):
        rs = pl.ds(h * hb, hb)
        light[0, rs, :] = jnp.zeros((hb, tile), F32)

        def add_light(k, carry):
            pr = probe[0, k, rs, :].astype(F32)
            pi = probe[1, k, rs, :].astype(F32)
            light[0, rs, :] = light[0, rs, :] + (pr * pr + pi * pi)
            return carry

        lax.fori_loop(0, modes, add_light, 0)
    light_copy = remote(
        light.at[0], light_in.at[0], (light_sem.at[0], light_sem.at[1]), other, idx
    )
    light_copy.start()

    for copy in table_copies:
        copy.wait()
    t1[0:tile, tile:] = -t1[tile:, 0:tile]
    t2[0:tile, 0:tile] = t1[0:tile, 0:tile]
    t2[0:tile, tile:] = t1[tile:, 0:tile]
    t2[tile:, 0:tile] = t1[0:tile, tile:]
    t2[tile:, tile:] = t1[0:tile, 0:tile]

    col = col_ref[0]
    moved = shift_ref[0].astype(F32)
    stays = 1.0 - moved
    halves = cols // hb
    strip = 32

    def hit(value, q):
        return jnp.maximum(1 - (value - q) * (value - q), 0)

    at_col = [hit(col, q).astype(F32) for q in range(halves - 1)]

    def window(ref, c, first):
        total = at_col[0] * ref[c, pl.ds(first, strip), pl.ds(0, tile)]
        for q in range(1, halves - 1):
            total = total + at_col[q] * ref[c, pl.ds(first, strip), pl.ds(q * hb, tile)]
        return total

    def exits(k, rs):
        pr = probe[0, k, rs, :].astype(F32)
        pi = probe[1, k, rs, :].astype(F32)
        o_r = patch[0, rs, :]
        o_i = patch[1, rs, :]
        er = (pr * o_r - pi * o_i).astype(BF16)
        ei = (pr * o_i + pi * o_r).astype(BF16)
        return pr, pi, o_r, o_i, er, ei

    for h in range(2):
        rs = pl.ds(h * hb, hb)
        if h == 1:
            rim_copy.wait()

        def gather(i, carry):
            here = pl.multiple_of(i * strip, strip)
            for c in range(2):
                if h == 0:
                    low = window(obj, c, hb + here)
                    top = window(obj, c, here)
                else:
                    low = jnp.where(idx == n - 1, 0.0, window(rim, c, here))
                    top = window(obj, c, hb + here)
                patch[c, pl.ds(h * hb + here, strip), :] = moved * low + stays * top
            return carry

        lax.fori_loop(0, hb // strip, gather, 0)

        def right(k, carry):
            er, ei = exits(k, rs)[4:]
            out = jnp.dot(
                jnp.concatenate([er, ei], axis=1), t1[...], preferred_element_type=F32
            ).astype(BF16)
            half[k, pl.ds(h * hb, hb), :] = out[:, :tile]
            half[k, pl.ds(tile + h * hb, hb), :] = out[:, tile:]
            return carry

        lax.fori_loop(0, modes, right, 0)

    light_copy.wait()
    lmax[...] = jnp.full(lmax.shape, jnp.max(light[0] + light_in[0]), F32)

    sum_copies = []
    for h in range(2):
        own_sum[h, 0:hb] = jnp.zeros((hb, tile), F32)

        def left(k, carry):
            wr = jnp.dot(t2[pl.ds(h * hb, hb), :], half[k], preferred_element_type=F32)
            wi = jnp.dot(t2[pl.ds(tile + h * hb, hb), :], half[k], preferred_element_type=F32)
            own_sum[h, 0:hb] = own_sum[h, 0:hb] + (wr * wr + wi * wi)
            for q in range(2):
                big[k, h, q, 0] = wr[q * quarter:(q + 1) * quarter].reshape(group, share, tile)
                big[k, h, q, 1] = wi[q * quarter:(q + 1) * quarter].reshape(group, share, tile)
            return carry

        lax.fori_loop(0, modes, left, 0)
        copy = remote(
            own_sum.at[h, pl.ds(0, hb)], peer_sum.at[h], (sum_sem.at[0, h], sum_sem.at[1, h]), other, idx
        )
        copy.start()
        sum_copies.append(copy)

    for h in range(2):
        sum_copies[h].wait()
        rs = pl.ds(h * hb, hb)
        total = jnp.maximum(own_sum[h, 0:hb] + peer_sum[h], 1.0)
        own_sum[h, 0:hb] = jnp.sqrt(pat[0, rs, :]) / jnp.sqrt(total)

        def fix(k, carry):
            scale = own_sum[h, 0:hb]
            parts = []
            for c in range(2):
                w = jnp.concatenate(
                    [big[k, h, q, c].reshape(quarter, tile) for q in range(2)], axis=0
                )
                parts.append((w * scale).astype(BF16))
            out = jnp.dot(
                jnp.concatenate(parts, axis=1), t2[...], preferred_element_type=F32
            ).astype(BF16)
            half[k, pl.ds(h * hb, hb), :] = out[:, :tile]
            half[k, pl.ds(tile + h * hb, hb), :] = out[:, tile:]
            return carry

        lax.fori_loop(0, modes, fix, 0)

    light[...] = jnp.zeros(light.shape, F32)

    def copy1(k):
        return remote(big.at[k, 1 - a], recv1.at[k], (sem1.at[0, k], sem1.at[1, k]), me, sib)

    def copy2(k):
        return remote(big.at[k, a, 1 - b], recv2.at[k], (sem2.at[0, k], sem2.at[1, k]), me, yid)

    def copy3(k, j):
        to = (m + j) % group
        return remote(
            big.at[k, a, b, :, to], recv3.at[k, j - 1],
            (sem3.at[0, k, j - 1], sem3.at[1, k, j - 1]), me, to * 4 + b * 2 + a,
        )

    def copy4(k):
        return remote(upd.at[k], upd_in.at[k], (sem4.at[0, k], sem4.at[1, k]), other, idx)

    def stage2(k):
        copy1(k).wait()
        big[k, a, 1 - b] = big[k, a, 1 - b] + recv1[k, 1 - b]
        copy2(k).start()
        big[k, a, b] = big[k, a, b] + recv1[k, b]

    def stage3(k):
        copy2(k).wait()
        big[k, a, b] = big[k, a, b] + recv2[k]
        for j in range(1, group):
            copy3(k, j).start()

    def stage4(k):
        total = big[k, a, b, :, m]
        for j in range(1, group):
            copy3(k, j).wait()
            total = total + recv3[k, j - 1]
        upd[k] = rows_in[k].astype(F32) + total / math.sqrt(positions)
        copy4(k).start()

    def step(k, carry):
        for h in range(2):
            rs = pl.ds(h * hb, hb)
            pr, pi, o_r, o_i, er, ei = exits(k, rs)
            rr = jnp.dot(t1[rs, :], half[k], preferred_element_type=F32) - er.astype(F32)
            ri = jnp.dot(
                t1[pl.ds(tile + h * hb, hb), :], half[k], preferred_element_type=F32
            ) - ei.astype(F32)
            light[0, rs, :] = light[0, rs, :] + (pr * rr + pi * ri)
            light[1, rs, :] = light[1, rs, :] + (pr * ri - pi * rr)
            grads = (o_r * rr + o_i * ri, o_r * ri - o_i * rr)
            for c in range(2):
                g = grads[c].reshape(group // 2, 2, 2, share, tile)
                for qb in range(2):
                    for qa in range(2):
                        big[k, qa, qb, c, pl.ds(h * (group // 2), group // 2)] = g[:, qb, qa]
        copy1(k).start()

        @pl.when(k >= 1)
        def _():
            stage2(k - 1)

        @pl.when(k >= 3)
        def _():
            stage3(k - 3)

        return carry

    lax.fori_loop(0, modes, step, 0)
    grad_copy = remote(light, light_in, (light_sem.at[2], light_sem.at[3]), other, idx)
    grad_copy.start()
    stage2(modes - 1)

    def drain(k, carry):
        stage3(k)
        stage4(k - modes + 3)
        return carry

    lax.fori_loop(modes - 3, modes, drain, 0)

    grad_copy.wait()
    light[...] = light[...] + light_in[...]
    own_sum[:, pl.ds(0, hb), :] = moved * light[:, pl.ds(hb, hb), :]
    own_sum[:, pl.ds(hb, 8), :] = jnp.full((2, 8, tile), col.astype(F32), F32)
    down_copy = remote(own_sum, down_in, (down_sem.at[0], down_sem.at[1]), me, nxt)
    down_copy.start()

    def finish(k, carry):
        stage4(k)
        return carry

    lax.fori_loop(3, modes, finish, 0)

    down_copy.wait()
    out_copies = []
    for c in range(2):
        for h in range(2):
            for z in range(2):
                rs = pl.ds(z * quarter, quarter)
                first = light[c, rs, :]
                if h == 0:
                    piece = stays * first / lmax[0:1, 0:1]
                    near = jnp.where(idx == 0, 0.0, down_in[c, rs, :]) / lmax[0:1, 0:1]
                    ncol = down_in[c, pl.ds(hb, 1), pl.ds(0, hb)]
                else:
                    second = light[c, pl.ds(hb + z * quarter, quarter), :]
                    piece = (stays * second + moved * first) / lmax[0:1, 0:1]
                for q in range(halves):
                    value = jnp.zeros((quarter, hb), F32)
                    if q < halves - 1:
                        value = at_col[q] * piece[:, :hb]
                        if h == 0:
                            value = value + hit(ncol, float(q)) * near[:, :hb]
                    if q > 0:
                        value = value + at_col[q - 1] * piece[:, hb:]
                        if h == 0:
                            value = value + hit(ncol, float(q - 1)) * near[:, hb:]
                    big[q // 2, h, z, c, :, :, pl.ds((q % 2) * hb, hb)] = value.reshape(
                        group, share, hb
                    )
            for z in range(2):
                for w in range(cols // tile):
                    copy = pltpu.make_async_copy(
                        big.at[w, h, z, c],
                        delta.at[c, pl.ds((h * 2 + z) * group, group), :, pl.ds(w * tile, tile)],
                        out_sem.at[c, h, z, w],
                    )
                    copy.start()
                    out_copies.append(copy)

    def arrived(k, carry):
        copy4(k).wait()
        return carry

    lax.fori_loop(0, modes, arrived, 0)
    for k in range(modes):
        acc = jnp.zeros((2, share, tile), F32)
        for j in range(modes):
            own = mix_ref[me * modes + k, me * modes + j].astype(F32) / 16.0
            far = mix_ref[me * modes + k, other * modes + j].astype(F32) / 16.0
            acc = acc + own * upd[j] + far * upd_in[j]
        for c in range(2):
            probe_new[c, k] = acc[c].astype(BF16)
    for copy in out_copies:
        copy.wait()


def per_device(object_field, probe, patterns, row_shift, col_start, mixing):
    tile = probe.shape[2]
    modes = probe.shape[1]
    cols = object_field.shape[2]
    n = lax.axis_size("scan")
    group = n // 4
    share = tile // n
    positions = patterns.shape[0] * n
    cosine, sine = tables(tile)
    hb = tile // 2
    dims = (n, group, share, tile, modes, positions, cols)
    row_start = lax.axis_index("scan") * share
    rows_in = lax.dynamic_slice_in_dim(probe, row_start, share, 2).transpose(1, 0, 2, 3)
    smem = pl.BlockSpec(memory_space=pltpu.SMEM)
    vmem = pl.BlockSpec(memory_space=pltpu.VMEM)
    dma = pltpu.SemaphoreType.DMA
    delta, probe_new = pl.pallas_call(
        functools.partial(kernel, dims),
        out_shape=(
            jax.ShapeDtypeStruct((2, tile // share, share, cols), F32),
            jax.ShapeDtypeStruct((2, modes, share, tile), BF16),
        ),
        in_specs=[smem, smem, smem] + [vmem] * 4 + [pl.BlockSpec(memory_space=pl.ANY)] * 2,
        out_specs=(pl.BlockSpec(memory_space=pl.ANY), vmem),
        scratch_shapes=[
            pltpu.VMEM((2, hb, cols), F32),
            pltpu.VMEM((2, tile, tile), F32),
            pltpu.VMEM((2 * tile, 2 * tile), BF16),
            pltpu.VMEM((2 * tile, 2 * tile), BF16),
            pltpu.VMEM((modes, 2 * tile, tile), BF16),
            pltpu.VMEM((modes, 2, 2, 2, group, share, tile), F32),
            pltpu.VMEM((modes, 2, 2, group, share, tile), F32),
            pltpu.VMEM((modes, 2, group, share, tile), F32),
            pltpu.VMEM((modes, group - 1, 2, share, tile), F32),
            pltpu.VMEM((2, tile, tile), F32),
            pltpu.VMEM((2, tile, tile), F32),
            pltpu.VMEM((2, hb + 8, tile), F32),
            pltpu.VMEM((2, hb, tile), F32),
            pltpu.VMEM((2, hb + 8, tile), F32),
            pltpu.VMEM((modes, 2, share, tile), F32),
            pltpu.VMEM((modes, 2, share, tile), F32),
            pltpu.VMEM((8, 128), F32),
            dma((2,)),
            dma((4,)),
            dma((2, 2)),
            dma((2, modes)),
            dma((2, modes)),
            dma((2, modes, group - 1)),
            dma((2, modes)),
            dma((2,)),
            dma((2, 2, 2, cols // tile)),
            dma((3,)),
        ],
        compiler_params=pltpu.CompilerParams(
            collective_id=0, has_side_effects=True, vmem_limit_bytes=67_000_000
        ),
    )(row_shift, col_start, mixing, object_field, probe, rows_in, patterns, cosine, sine)
    return (object_field + delta.reshape(object_field.shape), probe_new)


def solution(mesh):
    in_specs = (
        P(None, "scan", None),
        P(None, "mode", None, None),
        P("scan", None, None),
        P("scan"),
        P("scan"),
        P(),
    )
    out_specs = (P(None, "scan", None), P(None, "mode", "scan", None))
    return jax.shard_map(
        per_device, mesh=mesh, in_specs=in_specs, out_specs=out_specs, check_vma=False
    )
```
